32 devices in a mesh: tm: 4 (over y, x), stn: 8 (over z, core).
Axes of the slice: x: 2, y: 2, z: 4, core: 2. Of those that a mesh axis runs over, the one named last changes fastest.
Arguments:
- voltages: bfloat16 [2, 1024, 16384], P(None, 'stn', 'tm'), may hold values from -6 to 6
- filter_taps: float32 [12, 4096], replicated, may hold values from -1.75 to 1.75
- beam_weights: int32 [2, 512, 1024], P(None, 'stn'), may hold values from -32768 to 32767
- station_map: int32 [512], replicated, may hold values from 0 to 511, each once
- station_flags: int32 [512], replicated, may hold values 0 or 1
Outputs:
- beam_power: float32 [512, 4, 4096], P('stn', 'tm')
The draws below stay inside these ranges and needn't reach their ends.
Inputs may be any that keep to these rules, and one draw needn't show every extreme that they name: `station_map`: each station number appears once.
All inputs are finite; a program needn't handle non-finite values.
Results may differ from the reference program's by a relative error of at most 0.0039.
Values may be sent and summed in bfloat16 or wider, within the bound.
A program may use at most 64 MiB of HBM per device.

```python
import jax
import jax.numpy as jnp
from jax import lax

S = 512
B = 512
C = 4096
TAPS = 12
NIN = 1024
NFR = 4


def with_ends(values, own_key, low, high):
    longest = values.shape.index(max(values.shape))
    spots = []
    for shift in (0, 1):
        where = [jax.random.randint(jax.random.fold_in(own_key, axis), (), 0, length) for axis, length in enumerate(values.shape)]
        where[longest] = (where[longest] + shift) % values.shape[longest]
        spots.append(tuple(where))
    return values.at[spots[0]].set(low).at[spots[1]].set(high)


def level_of(own_key, extent, cuts, low, top_value):
    loudness = 1.0
    for dim, parts in cuts:
        steps = jax.random.uniform(jax.random.fold_in(jax.random.fold_in(own_key, 6), dim), (parts,), jnp.float32, low / len(cuts), top_value / len(cuts))
        loudness = loudness * jnp.repeat(jnp.exp(steps), extent[dim] // parts).reshape((-1,) + (1,) * (len(extent) - 1 - dim))
    return loudness


def gaussian(rng, shape, scale, bound, shards=(), held_as=jnp.bfloat16):
    array = jax.random.normal(rng, shape, jnp.float32) * scale
    if len(shards) > 0:
        array = level_of(rng, shape, shards, -0.22, 0.18) * array
    return jnp.clip(array, min=-bound, max=bound).astype(held_as)


def setup_inputs(seed: int = 0) -> dict:
    key_of = jax.random.split(jax.random.key(seed), 6)
    voltages = gaussian(key_of[0], (2, NIN, NFR * C), 1.0, 6.0, ((1, 8), (2, 4)))
    filter_taps = gaussian(key_of[1], (TAPS, C), TAPS ** -0.5, 1.75, (), jnp.float32)
    beam_weights = with_ends(jax.random.randint(key_of[2], (2, B, NIN), -32768, 32768), jax.random.fold_in(key_of[2], 1), -32768, 32767).astype(jnp.int32)
    station_map = jax.random.permutation(key_of[3], S).astype(jnp.int32)
    station_flags = with_ends((jax.random.randint(key_of[4], (S,), 0, 8) < 7).astype(jnp.int32), jax.random.fold_in(key_of[4], 1), 0, 1)
    return dict(voltages=voltages, filter_taps=filter_taps, beam_weights=beam_weights, station_map=station_map, station_flags=station_flags)


def reference(voltages, filter_taps, beam_weights, station_map, station_flags):
    flag_slot = station_flags[station_map]
    keep_mask = jnp.repeat(flag_slot, 2).astype(voltages.dtype)
    masked = voltages * keep_mask[None, :, None]
    frames = masked.reshape(2, NIN, NFR, C)
    padded = jnp.concatenate([jnp.zeros((2, NIN, TAPS - 1, C), frames.dtype), frames], axis=2)
    weight_int = beam_weights.reshape(2, B, S, 2)[:, :, station_map, :].reshape(2, B, NIN)
    weight_low = (weight_int.astype(jnp.float32) * (1.0 / 32768.0)).astype(jnp.bfloat16)
    weight_full = lax.optimization_barrier(weight_low).astype(jnp.float32)

    def per_frame(frame_index):
        window = lax.dynamic_slice_in_dim(padded, frame_index, TAPS, 2).astype(jnp.float32)
        filtered = lax.optimization_barrier(jnp.sum(window * filter_taps[None, None, :, :], axis=2))
        spectrum = jnp.fft.fft(lax.complex(filtered[0], filtered[1]), axis=-1) / jnp.sqrt(jnp.float32(C))
        chan_real = lax.optimization_barrier(jnp.real(spectrum).astype(jnp.bfloat16)).astype(jnp.float32)
        chan_imag = lax.optimization_barrier(jnp.imag(spectrum).astype(jnp.bfloat16)).astype(jnp.float32)
        beam_real = jnp.dot(weight_full[0], chan_real) - jnp.dot(weight_full[1], chan_imag)
        beam_imag = jnp.dot(weight_full[0], chan_imag) + jnp.dot(weight_full[1], chan_real)
        return (beam_real * beam_real + beam_imag * beam_imag) / NIN
    power_all = lax.map(per_frame, jnp.arange(NFR, dtype=jnp.int32))
    return jnp.transpose(power_all, (1, 0, 2))
```

```python
import functools
import math

import jax
import jax.numpy as jnp
import numpy as np
from jax import lax
from jax.experimental import pallas as pl
from jax.experimental.pallas import tpu as pltpu
from jax.sharding import PartitionSpec as P

LANES = 128


def fft_list(re, im):
    size = len(re)
    if size == 1:
        return re, im
    even_re, even_im = fft_list(re[0::2], im[0::2])
    odd_re, odd_im = fft_list(re[1::2], im[1::2])
    half = size // 2
    out_re, out_im = [None] * size, [None] * size
    for k in range(half):
        a, b = odd_re[k], odd_im[k]
        if k == 0:
            tr, ti = a, b
        elif 4 * k == size:
            tr, ti = b, -a
        elif 8 * k == size:
            h = math.sqrt(0.5)
            tr, ti = (a + b) * h, (b - a) * h
        elif 8 * k == 3 * size:
            h = math.sqrt(0.5)
            tr, ti = (b - a) * h, (a + b) * (-h)
        else:
            c, s = math.cos(2 * math.pi * k / size), math.sin(2 * math.pi * k / size)
            tr, ti = a * c + b * s, b * c - a * s
        out_re[k], out_re[k + half] = even_re[k] + tr, even_re[k] - tr
        out_im[k], out_im[k + half] = even_im[k] + ti, even_im[k] - ti
    return out_re, out_im


def spectra_kernel(radix, groups, rows, x_ref, taps_ref, twr_ref, twi_ref, th_ref, tl_ref, o_ref, mid_ref, y_ref):
    frames = x_ref.shape[1]
    inputs = x_ref.shape[2]
    taps = taps_ref.shape[0]
    lags = min(taps, frames)
    sub = radix // 4
    per_group = radix // groups
    blocks = inputs // rows

    def unit(step, carry):
        n = step // blocks
        block = step % blocks
        start = block * rows
        if rows % 16 == 0:
            start = pl.multiple_of(start, rows)
        gates = [jnp.where(n >= lag, 1.0, 0.0).astype(jnp.float32) for lag in range(lags)]
        index = [jnp.maximum(n - lag, 0) for lag in range(lags)]
        for a in range(4):
            tile_re, tile_im = [], []
            for j in range(sub):
                c1 = a + 4 * j
                cols = slice(c1 * LANES, (c1 + 1) * LANES)
                acc_re = acc_im = None
                for lag in range(lags):
                    tap = taps_ref[taps - 1 - lag : taps - lag, cols]
                    if lag:
                        tap = tap * gates[lag]
                    pr = x_ref[0, index[lag], pl.ds(start, rows), cols].astype(jnp.float32) * tap
                    pi = x_ref[1, index[lag], pl.ds(start, rows), cols].astype(jnp.float32) * tap
                    acc_re = pr if acc_re is None else acc_re + pr
                    acc_im = pi if acc_im is None else acc_im + pi
                tile_re.append(acc_re)
                tile_im.append(acc_im)
            out_re, out_im = fft_list(tile_re, tile_im)
            for q in range(sub):
                if a * q:
                    c = math.cos(2 * math.pi * a * q / radix)
                    s = math.sin(2 * math.pi * a * q / radix)
                    mid_ref[0, a * sub + q] = out_re[q] * c + out_im[q] * s
                    mid_ref[1, a * sub + q] = out_im[q] * c - out_re[q] * s
                else:
                    mid_ref[0, a * sub + q] = out_re[q]
                    mid_ref[1, a * sub + q] = out_im[q]
        for q in range(sub):
            out_re, out_im = fft_list(
                [mid_ref[0, a * sub + q] for a in range(4)], [mid_ref[1, a * sub + q] for a in range(4)]
            )
            for r in range(4):
                k1 = q + sub * r
                c = twr_ref[k1 : k1 + 1, :]
                s = twi_ref[k1 : k1 + 1, :]
                y_ref[k1 * rows : (k1 + 1) * rows, 0:LANES] = out_re[r] * c + out_im[r] * s
                y_ref[k1 * rows : (k1 + 1) * rows, LANES : 2 * LANES] = out_im[r] * c - out_re[r] * s
        y = y_ref[...]
        high = y.astype(jnp.bfloat16)
        low = (y - high.astype(jnp.float32)).astype(jnp.bfloat16)
        out = (
            jnp.dot(high, th_ref[...], preferred_element_type=jnp.float32)
            + jnp.dot(low, th_ref[...], preferred_element_type=jnp.float32)
            + jnp.dot(high, tl_ref[...], preferred_element_type=jnp.float32)
        ).astype(jnp.bfloat16)
        for k1 in range(radix):
            group, kk = k1 // per_group, k1 % per_group
            for p in range(2):
                o_ref[n * groups + group, p, pl.ds(start, rows), kk * LANES : (kk + 1) * LANES] = out[
                    k1 * rows : (k1 + 1) * rows, p * LANES : (p + 1) * LANES
                ]
        return carry

    lax.fori_loop(0, frames * blocks, unit, 0)


def make_spectra(x, filter_taps, groups):
    _, frames, inputs, channels = x.shape
    radix = channels // LANES
    rows = math.gcd(16, inputs)
    k1 = np.arange(radix)[:, None]
    c2 = np.arange(LANES)
    turn = 2.0 * np.pi * (k1 * c2[None, :]) / channels
    twr, twi = np.cos(turn).astype(np.float32), np.sin(turn).astype(np.float32)
    angle = 2.0 * np.pi * ((c2[:, None] * c2[None, :]) % LANES) / LANES
    cos, sin = np.cos(angle), np.sin(angle)
    table = (np.block([[cos, -sin], [sin, cos]]) / math.sqrt(channels)).astype(np.float32)
    table_high = table.astype(jnp.bfloat16)
    table_low = (table - table_high.astype(np.float32)).astype(jnp.bfloat16)
    return pl.pallas_call(
        functools.partial(spectra_kernel, radix, groups, rows),
        out_shape=jax.ShapeDtypeStruct(
            (frames * groups, 2, inputs, channels // groups), jnp.bfloat16
        ),
        in_specs=[pl.BlockSpec(memory_space=pltpu.VMEM)] * 6,
        out_specs=pl.BlockSpec(memory_space=pltpu.VMEM),
        scratch_shapes=[
            pltpu.VMEM((2, radix, rows, LANES), jnp.float32),
            pltpu.VMEM((radix * rows, 2 * LANES), jnp.float32),
        ],
    )(x, filter_taps, twr, twi, table_high, table_low)


def beam_kernel(scale, x_ref, w_ref, o_ref):
    groups, _, rows, width = x_ref.shape
    x_re = x_ref[:, 0].reshape(groups * rows, width)
    x_im = x_ref[:, 1].reshape(groups * rows, width)

    def block(step, carry):
        size = o_ref.shape[0] // 4
        start = pl.multiple_of(step * size, size)
        w_re = w_ref[0, pl.ds(start, size), :]
        w_im = w_ref[1, pl.ds(start, size), :]
        beam_re = jnp.dot(w_re, x_re, preferred_element_type=jnp.float32) - jnp.dot(
            w_im, x_im, preferred_element_type=jnp.float32
        )
        beam_im = jnp.dot(w_re, x_im, preferred_element_type=jnp.float32) + jnp.dot(
            w_im, x_re, preferred_element_type=jnp.float32
        )
        power = (beam_re * beam_re + beam_im * beam_im) * scale
        o_ref[pl.ds(start, size), :] = power.astype(jnp.bfloat16)
        return carry

    lax.fori_loop(0, 4, block, 0)


def make_power(spectra, weights):
    inputs_all = weights.shape[2]
    if spectra.shape[2] % 16:
        spectra = spectra.transpose(1, 0, 2, 3).reshape(1, 2, inputs_all, spectra.shape[3])
    return pl.pallas_call(
        functools.partial(beam_kernel, 1.0 / inputs_all),
        out_shape=jax.ShapeDtypeStruct((weights.shape[1], spectra.shape[3]), jnp.bfloat16),
        in_specs=[pl.BlockSpec(memory_space=pltpu.VMEM)] * 2,
        out_specs=pl.BlockSpec(memory_space=pltpu.VMEM),
    )(spectra, weights)


def local_weights(beam_weights, station_map, station_flags, tm_size, stn_size):
    inputs_all = beam_weights.shape[2]
    few = inputs_all // (tm_size * stn_size)
    column = jnp.arange(inputs_all, dtype=jnp.int32)
    source, inner = column // few, column % few
    slot_input = (source % stn_size) * (few * tm_size) + (source // stn_size) * few + inner
    flag = station_flags[station_map]
    wanted = (2 * station_map[slot_input // 2] + slot_input % 2).astype(jnp.int32)
    keep = flag[slot_input // 2]
    pick = (jnp.arange(inputs_all, dtype=jnp.int32)[:, None] == wanted[None, :]) & (keep[None, :] != 0)
    low = (beam_weights.astype(jnp.float32) * (1.0 / 32768.0)).astype(jnp.bfloat16)
    return jnp.dot(
        low.reshape(-1, inputs_all), pick.astype(jnp.bfloat16), preferred_element_type=jnp.float32
    ).astype(jnp.bfloat16).reshape(low.shape)


def on_device(tm_size, stn_size, voltages, filter_taps, beam_weights, station_map, station_flags):
    channels = filter_taps.shape[1]
    few = voltages.shape[1] // tm_size
    weights = local_weights(beam_weights, station_map, station_flags, tm_size, stn_size)
    weight_all = lax.all_gather(weights, "stn", axis=1, tiled=True)
    frames = voltages.reshape(2, tm_size, few, channels)
    frames = lax.all_to_all(frames, "tm", split_axis=1, concat_axis=1, tiled=True)
    spectra = make_spectra(frames, filter_taps, stn_size)
    turned = lax.all_to_all(spectra, ("tm", "stn"), split_axis=0, concat_axis=0, tiled=True)
    power = make_power(turned, weight_all)
    beams = power.shape[0] // stn_size
    mine = lax.all_to_all(
        power.reshape(stn_size, beams, -1), "stn", split_axis=0, concat_axis=0, tiled=True
    )
    radix = channels // LANES
    mine = mine.reshape(stn_size, beams, radix // stn_size, LANES).astype(jnp.float32)
    return mine.transpose(1, 3, 0, 2).reshape(beams, 1, channels)


def solution(mesh):
    placed = (P(None, "stn", "tm"), P(), P(None, "stn", None), P(), P())
    body = functools.partial(on_device, mesh.shape["tm"], mesh.shape["stn"])
    return jax.shard_map(
        body, mesh=mesh, in_specs=placed, out_specs=P("stn", "tm", None), check_vma=False
    )
```

```python
import functools
import math

import jax
import jax.numpy as jnp
import numpy as np
from jax import lax
from jax.experimental import pallas as pl
from jax.experimental.pallas import tpu as pltpu
from jax.sharding import PartitionSpec as P

LANES = 128


def fft_list(re, im):
    size = len(re)
    if size == 1:
        return re, im
    even_re, even_im = fft_list(re[0::2], im[0::2])
    odd_re, odd_im = fft_list(re[1::2], im[1::2])
    half = size // 2
    out_re, out_im = [None] * size, [None] * size
    for k in range(half):
        a, b = odd_re[k], odd_im[k]
        if k == 0:
            tr, ti = a, b
        elif 4 * k == size:
            tr, ti = b, -a
        elif 8 * k == size:
            h = math.sqrt(0.5)
            tr, ti = (a + b) * h, (b - a) * h
        elif 8 * k == 3 * size:
            h = math.sqrt(0.5)
            tr, ti = (b - a) * h, (a + b) * (-h)
        else:
            c, s = math.cos(2 * math.pi * k / size), math.sin(2 * math.pi * k / size)
            tr, ti = a * c + b * s, b * c - a * s
        out_re[k], out_re[k + half] = even_re[k] + tr, even_re[k] - tr
        out_im[k], out_im[k + half] = even_im[k] + ti, even_im[k] - ti
    return out_re, out_im


def transform_unit(radix, rows, frames, n, load, store, taps_ref, twr_ref, twi_ref, th_ref, tl_ref, mid_ref, y_ref):
    taps = taps_ref.shape[0]
    lags = min(taps, frames)
    sub = radix // 4
    gates = [jnp.where(n >= lag, 1.0, 0.0).astype(jnp.float32) for lag in range(lags)]
    index = [jnp.maximum(n - lag, 0) for lag in range(lags)]
    for a in range(4):
        tile_re, tile_im = [], []
        for j in range(sub):
            c1 = a + 4 * j
            cols = slice(c1 * LANES, (c1 + 1) * LANES)
            acc_re = acc_im = None
            for lag in range(lags):
                tap = taps_ref[taps - 1 - lag : taps - lag, cols]
                if lag:
                    tap = tap * gates[lag]
                pr = load(0, index[lag], cols).astype(jnp.float32) * tap
                pi = load(1, index[lag], cols).astype(jnp.float32) * tap
                acc_re = pr if acc_re is None else acc_re + pr
                acc_im = pi if acc_im is None else acc_im + pi
            tile_re.append(acc_re)
            tile_im.append(acc_im)
        out_re, out_im = fft_list(tile_re, tile_im)
        for q in range(sub):
            if a * q:
                c = math.cos(2 * math.pi * a * q / radix)
                s = math.sin(2 * math.pi * a * q / radix)
                mid_ref[0, a * sub + q] = out_re[q] * c + out_im[q] * s
                mid_ref[1, a * sub + q] = out_im[q] * c - out_re[q] * s
            else:
                mid_ref[0, a * sub + q] = out_re[q]
                mid_ref[1, a * sub + q] = out_im[q]
    for q in range(sub):
        out_re, out_im = fft_list(
            [mid_ref[0, a * sub + q] for a in range(4)], [mid_ref[1, a * sub + q] for a in range(4)]
        )
        for r in range(4):
            k1 = q + sub * r
            c = twr_ref[k1 : k1 + 1, :]
            s = twi_ref[k1 : k1 + 1, :]
            y_ref[k1 * rows : (k1 + 1) * rows, 0:LANES] = out_re[r] * c + out_im[r] * s
            y_ref[k1 * rows : (k1 + 1) * rows, LANES : 2 * LANES] = out_im[r] * c - out_re[r] * s
    y = y_ref[...]
    high = y.astype(jnp.bfloat16)
    low = (y - high.astype(jnp.float32)).astype(jnp.bfloat16)
    out = (
        jnp.dot(high, th_ref[...], preferred_element_type=jnp.float32)
        + jnp.dot(low, th_ref[...], preferred_element_type=jnp.float32)
        + jnp.dot(high, tl_ref[...], preferred_element_type=jnp.float32)
    ).astype(jnp.bfloat16)
    for k1 in range(radix):
        for p in range(2):
            store(k1, p, out[k1 * rows : (k1 + 1) * rows, p * LANES : (p + 1) * LANES])


def spectra_kernel(radix, groups, rows, x_ref, taps_ref, twr_ref, twi_ref, th_ref, tl_ref, o_ref, mid_ref, y_ref):
    frames = x_ref.shape[1]
    blocks = x_ref.shape[2] // rows
    per_group = radix // groups

    def unit(step, carry):
        n = step // blocks
        start = step % blocks * rows
        if rows % 16 == 0:
            start = pl.multiple_of(start, rows)

        def load(p, frame, cols):
            return x_ref[p, frame, pl.ds(start, rows), cols]

        def store(k1, p, value):
            kk = k1 % per_group
            o_ref[n * groups + k1 // per_group, p, pl.ds(start, rows), kk * LANES : (kk + 1) * LANES] = value

        transform_unit(
            radix, rows, frames, n, load, store, taps_ref, twr_ref, twi_ref, th_ref, tl_ref, mid_ref, y_ref
        )
        return carry

    lax.fori_loop(0, frames * blocks, unit, 0)


def tables(channels):
    radix = channels // LANES
    k1 = np.arange(radix)[:, None]
    c2 = np.arange(LANES)
    turn = 2.0 * np.pi * (k1 * c2[None, :]) / channels
    twr, twi = np.cos(turn).astype(np.float32), np.sin(turn).astype(np.float32)
    angle = 2.0 * np.pi * ((c2[:, None] * c2[None, :]) % LANES) / LANES
    cos, sin = np.cos(angle), np.sin(angle)
    table = (np.block([[cos, -sin], [sin, cos]]) / math.sqrt(channels)).astype(np.float32)
    table_high = table.astype(jnp.bfloat16)
    table_low = (table - table_high.astype(np.float32)).astype(jnp.bfloat16)
    return twr, twi, table_high, table_low


def make_spectra(x, filter_taps, groups):
    _, frames, inputs, channels = x.shape
    radix = channels // LANES
    rows = math.gcd(16, inputs)
    return pl.pallas_call(
        functools.partial(spectra_kernel, radix, groups, rows),
        out_shape=jax.ShapeDtypeStruct(
            (frames * groups, 2, inputs, channels // groups), jnp.bfloat16
        ),
        in_specs=[pl.BlockSpec(memory_space=pltpu.VMEM)] * 6,
        out_specs=pl.BlockSpec(memory_space=pltpu.VMEM),
        scratch_shapes=[
            pltpu.VMEM((2, radix, rows, LANES), jnp.float32),
            pltpu.VMEM((radix * rows, 2 * LANES), jnp.float32),
        ],
    )(x, filter_taps, *tables(channels))


def beam_kernel(scale, x_ref, w_ref, o_ref):
    groups, _, rows, width = x_ref.shape
    x_re = x_ref[:, 0].reshape(groups * rows, width)
    x_im = x_ref[:, 1].reshape(groups * rows, width)

    def block(step, carry):
        size = o_ref.shape[0] // 4
        start = pl.multiple_of(step * size, size)
        w_re = w_ref[0, pl.ds(start, size), :]
        w_im = w_ref[1, pl.ds(start, size), :]
        beam_re = jnp.dot(w_re, x_re, preferred_element_type=jnp.float32) - jnp.dot(
            w_im, x_im, preferred_element_type=jnp.float32
        )
        beam_im = jnp.dot(w_re, x_im, preferred_element_type=jnp.float32) + jnp.dot(
            w_im, x_re, preferred_element_type=jnp.float32
        )
        power = (beam_re * beam_re + beam_im * beam_im) * scale
        o_ref[pl.ds(start, size), :] = power.astype(jnp.bfloat16)
        return carry

    lax.fori_loop(0, 4, block, 0)


def make_power(spectra, weights):
    inputs_all = weights.shape[2]
    if spectra.shape[2] % 16:
        spectra = spectra.transpose(1, 0, 2, 3).reshape(1, 2, inputs_all, spectra.shape[3])
    return pl.pallas_call(
        functools.partial(beam_kernel, 1.0 / inputs_all),
        out_shape=jax.ShapeDtypeStruct((weights.shape[1], spectra.shape[3]), jnp.bfloat16),
        in_specs=[pl.BlockSpec(memory_space=pltpu.VMEM)] * 2,
        out_specs=pl.BlockSpec(memory_space=pltpu.VMEM),
    )(spectra, weights)


def local_weights(beam_weights, station_map, station_flags, tm_size, stn_size):
    inputs_all = beam_weights.shape[2]
    few = inputs_all // (tm_size * stn_size)
    column = jnp.arange(inputs_all, dtype=jnp.int32)
    source, inner = column // few, column % few
    slot_input = (source % stn_size) * (few * tm_size) + (source // stn_size) * few + inner
    flag = station_flags[station_map]
    wanted = (2 * station_map[slot_input // 2] + slot_input % 2).astype(jnp.int32)
    keep = flag[slot_input // 2]
    pick = (jnp.arange(inputs_all, dtype=jnp.int32)[:, None] == wanted[None, :]) & (keep[None, :] != 0)
    low = (beam_weights.astype(jnp.float32) * (1.0 / 32768.0)).astype(jnp.bfloat16)
    return jnp.dot(
        low.reshape(-1, inputs_all), pick.astype(jnp.bfloat16), preferred_element_type=jnp.float32
    ).astype(jnp.bfloat16).reshape(low.shape)


def fused_kernel(
    tm, stn, radix, scale,
    v_ref, w_ref, wanted_ref, flag_ref, taps_ref, twr_ref, twi_ref, th_ref, tl_ref,
    o_ref,
    xbuf, sbuf, rbuf, wbuf, acc, pbuf, qbuf, mid_ref, y_ref,
    v_send, v_recv, up_send, up_recv, down_send, down_recv, side_send, side_recv,
    s_send, s_recv, p_send, p_recv, o_sem,
):
    halves, rows = xbuf.shape[0], xbuf.shape[3]
    chips = stn // 2
    per_group = radix // stn
    me_t, me_s = lax.axis_index("tm"), lax.axis_index("stn")
    z, core = me_s // 2, me_s % 2
    me = me_t * stn + me_s
    width = rbuf.shape[4]

    def remote(src, dst, send, recv, t, s):
        return pltpu.make_async_remote_copy(
            src_ref=src, dst_ref=dst, send_sem=send, recv_sem=recv,
            device_id=(t, s), device_id_type=pl.DeviceIdType.MESH,
        )

    def settle(ref, sem):
        pltpu.make_async_copy(ref, ref, sem).wait()

    barrier = pltpu.get_barrier_semaphore()

    def greet(d, carry):
        other = lax.rem(me + d, tm * stn)
        pl.semaphore_signal(
            barrier, inc=1, device_id=(other // stn, other % stn), device_id_type=pl.DeviceIdType.MESH
        )
        return carry

    lax.fori_loop(1, tm * stn, greet, 0)
    pl.semaphore_wait(barrier, tm * stn - 1)

    for h in range(halves):
        for d in range(1, tm):
            t = lax.rem(me_t + d, tm)
            remote(
                v_ref.at[:, t, h * rows : (h + 1) * rows], xbuf.at[h, :, me_t],
                v_send.at[h], v_recv.at[h], t, me_s,
            ).start()
        pltpu.make_async_copy(
            v_ref.at[:, me_t, h * rows : (h + 1) * rows], xbuf.at[h, :, me_t], v_recv.at[h]
        ).start()

    beams, inputs_all = w_ref.shape[1], w_ref.shape[2]
    low = (w_ref[...].astype(jnp.float32) * (flag_ref[...] * (1.0 / 32768.0))[None]).astype(jnp.bfloat16)
    low = low.reshape(2 * beams, inputs_all)
    step = min(256, inputs_all)
    for first in range(0, inputs_all, step):
        station = lax.broadcasted_iota(jnp.int32, (inputs_all, step), 0)
        pick = jnp.where(station == wanted_ref[:, first : first + step], 1.0, 0.0).astype(jnp.bfloat16)
        wbuf[me_s, :, first : first + step] = jnp.dot(
            low, pick, preferred_element_type=jnp.float32
        ).astype(jnp.bfloat16)

    def to_side(block):
        slot = 2 * block + core
        remote(wbuf.at[slot], wbuf.at[slot], side_send.at[block], side_recv.at[block], me_t, 2 * z + 1 - core).start()

    def chain_send(r):
        @pl.when((z >= r) & (z < chips - 1))
        def _():
            slot = 2 * (z - r) + core
            remote(wbuf.at[slot], wbuf.at[slot], up_send.at[r], up_recv.at[r], me_t, me_s + 2).start()

        @pl.when((z + r <= chips - 1) & (z > 0))
        def _():
            slot = 2 * (z + r) + core
            remote(wbuf.at[slot], wbuf.at[slot], down_send.at[r], down_recv.at[r], me_t, me_s - 2).start()

    def chain_recv(r):
        @pl.when(z - 1 - r >= 0)
        def _():
            settle(wbuf.at[0], up_recv.at[r])
            to_side(z - 1 - r)

        @pl.when(z + 1 + r <= chips - 1)
        def _():
            settle(wbuf.at[0], down_recv.at[r])
            to_side(z + 1 + r)

    to_side(z)
    chain_send(0)
    for r in range(1, chips - 1):
        if r < chips - 2:
            chain_recv(r - 1)
            chain_send(r)

    for h in range(halves):
        settle(xbuf.at[h], v_recv.at[h])

        def frame(j, carry):
            n = lax.rem(me_t + j, tm)

            def load(p, index, cols):
                return xbuf[h, p, index, :, cols]

            def store(k1, p, value):
                kk = k1 % per_group
                sbuf[h, n * stn + k1 // per_group, p, :, kk * LANES : (kk + 1) * LANES] = value

            transform_unit(
                radix, rows, tm, n, load, store, taps_ref, twr_ref, twi_ref, th_ref, tl_ref, mid_ref, y_ref
            )

            def send(e, inner):
                s = lax.rem(me_s + e, stn)
                remote(
                    sbuf.at[h, n * stn + s], rbuf.at[h, me], s_send.at[h], s_recv.at[h], n, s
                ).start()
                return inner

            lax.fori_loop(1, stn, send, 0)

            @pl.when(j > 0)
            def _():
                send(0, 0)

            @pl.when(j == 0)
            def _():
                pltpu.make_async_copy(sbuf.at[h, me], rbuf.at[h, me], s_recv.at[h]).start()

            return carry

        lax.fori_loop(0, tm, frame, 0)
        if h == 0:
            if chips > 2:
                chain_recv(chips - 3)
                chain_send(chips - 2)
    if chips > 1:
        chain_recv(chips - 2)

    for block in range(chips):
        settle(wbuf.at[0], side_recv.at[block])

    def beams_of(h, pair):
        cols = slice(h * inputs_all // halves, (h + 1) * inputs_all // halves)
        w = wbuf[pl.ds(2 * pair, 2), :, cols].reshape(4 * beams, inputs_all // halves)
        x_re = rbuf[h, :, 0].reshape(inputs_all // halves, width)
        x_im = rbuf[h, :, 1].reshape(inputs_all // halves, width)
        by_re = jnp.dot(w, x_re, preferred_element_type=jnp.float32).reshape(2, 2, beams, width)
        by_im = jnp.dot(w, x_im, preferred_element_type=jnp.float32).reshape(2, 2, beams, width)
        return by_re[:, 0] - by_im[:, 1], by_im[:, 0] + by_re[:, 1]

    for h in range(halves - 1):
        settle(rbuf.at[h], s_recv.at[h])

        def collect(pair, carry):
            beam_re, beam_im = beams_of(h, pair)
            two = pl.ds(2 * pair, 2)
            if h:
                beam_re, beam_im = beam_re + acc[0, two], beam_im + acc[1, two]
            acc[0, two] = beam_re
            acc[1, two] = beam_im
            return carry

        lax.fori_loop(0, chips, collect, 0)

    settle(rbuf.at[halves - 1], s_recv.at[halves - 1])

    def finish(i, carry):
        pair = lax.rem(z + 1 + i, chips)
        beam_re, beam_im = beams_of(halves - 1, pair)
        two = pl.ds(2 * pair, 2)
        if halves > 1:
            beam_re, beam_im = beam_re + acc[0, two], beam_im + acc[1, two]
        qbuf[two] = ((beam_re * beam_re + beam_im * beam_im) * scale).astype(jnp.bfloat16)
        other = 2 * pair + 1 - core
        same = 2 * pair + core
        remote(qbuf.at[other], pbuf.at[me_s], p_send, p_recv, me_t, other).start()

        @pl.when(i < chips - 1)
        def _():
            remote(qbuf.at[same], pbuf.at[me_s], p_send, p_recv, me_t, same).start()

        @pl.when(i == chips - 1)
        def _():
            pltpu.make_async_copy(qbuf.at[me_s], pbuf.at[me_s], p_recv).start()

        return carry

    lax.fori_loop(0, chips, finish, 0)

    for h in range(halves):
        settle(xbuf.at[h, :, 0 : tm - 1], v_send.at[h])
        settle(sbuf.at[h, 0 : tm * stn - 1], s_send.at[h])
    for block in range(chips):
        settle(wbuf.at[0], side_send.at[block])
    for r in range(chips - 1):
        @pl.when((z >= r) & (z < chips - 1))
        def _():
            settle(wbuf.at[0], up_send.at[r])

        @pl.when((z + r <= chips - 1) & (z > 0))
        def _():
            settle(wbuf.at[0], down_send.at[r])
    settle(qbuf.at[0 : stn - 1], p_send)
    settle(pbuf, p_recv)
    out = pltpu.make_async_copy(pbuf, o_ref, o_sem)
    out.start()
    out.wait()


def fused(tm, stn, voltages, filter_taps, beam_weights, station_map, station_flags):
    channels = filter_taps.shape[1]
    radix = channels // LANES
    few = voltages.shape[1] // tm
    halves = 2
    rows = few // halves
    width = channels // stn
    beams, inputs_all = beam_weights.shape[1], beam_weights.shape[2]
    chips = stn // 2
    wanted = (2 * station_map[:, None] + jnp.arange(2, dtype=jnp.int32)[None, :]).reshape(
        stn, tm, halves, rows
    ).transpose(2, 1, 0, 3).reshape(1, inputs_all)
    flags = jnp.repeat(station_flags, 2).astype(jnp.float32).reshape(1, inputs_all)
    dma = pltpu.SemaphoreType.DMA
    vmem = pl.BlockSpec(memory_space=pltpu.VMEM)
    hbm = pl.BlockSpec(memory_space=pl.ANY)
    low = jnp.bfloat16
    return pl.pallas_call(
        functools.partial(fused_kernel, tm, stn, radix, 1.0 / inputs_all),
        out_shape=jax.ShapeDtypeStruct((stn, beams, width), low),
        in_specs=[hbm] + [vmem] * 8,
        out_specs=hbm,
        scratch_shapes=[
            pltpu.VMEM((halves, 2, tm, rows, channels), low),
            pltpu.VMEM((halves, tm * stn, 2, rows, width), low),
            pltpu.VMEM((halves, tm * stn, 2, rows, width), low),
            pltpu.VMEM((stn, 2 * beams, inputs_all), low),
            pltpu.VMEM((2, stn, beams, width), jnp.float32),
            pltpu.VMEM((stn, beams, width), low),
            pltpu.VMEM((stn, beams, width), low),
            pltpu.VMEM((2, radix, rows, LANES), jnp.float32),
            pltpu.VMEM((radix * rows, 2 * LANES), jnp.float32),
            dma((halves,)), dma((halves,)),
            dma((chips,)), dma((chips,)), dma((chips,)), dma((chips,)), dma((chips,)), dma((chips,)),
            dma((halves,)), dma((halves,)), dma, dma, dma,
        ],
        compiler_params=pltpu.CompilerParams(collective_id=0, has_side_effects=True),
    )(
        voltages.reshape(2, tm, few, channels), beam_weights, wanted, flags, filter_taps, *tables(channels)
    )


def on_device(tm_size, stn_size, voltages, filter_taps, beam_weights, station_map, station_flags):
    channels = filter_taps.shape[1]
    few = voltages.shape[1] // tm_size
    if few % 32 == 0 and stn_size % 2 == 0:
        mine = fused(tm_size, stn_size, voltages, filter_taps, beam_weights, station_map, station_flags)
        beams = mine.shape[1]
    else:
        weights = local_weights(beam_weights, station_map, station_flags, tm_size, stn_size)
        weight_all = lax.all_gather(weights, "stn", axis=1, tiled=True)
        frames = voltages.reshape(2, tm_size, few, channels)
        frames = lax.all_to_all(frames, "tm", split_axis=1, concat_axis=1, tiled=True)
        spectra = make_spectra(frames, filter_taps, stn_size)
        turned = lax.all_to_all(spectra, ("tm", "stn"), split_axis=0, concat_axis=0, tiled=True)
        power = make_power(turned, weight_all)
        beams = power.shape[0] // stn_size
        mine = lax.all_to_all(
            power.reshape(stn_size, beams, -1), "stn", split_axis=0, concat_axis=0, tiled=True
        )
    radix = channels // LANES
    mine = mine.reshape(stn_size, beams, radix // stn_size, LANES).astype(jnp.float32)
    return mine.transpose(1, 3, 0, 2).reshape(beams, 1, channels)


def solution(mesh):
    placed = (P(None, "stn", "tm"), P(), P(None, "stn", None), P(), P())
    body = functools.partial(on_device, mesh.shape["tm"], mesh.shape["stn"])
    return jax.shard_map(
        body, mesh=mesh, in_specs=placed, out_specs=P("stn", "tm", None), check_vma=False
    )
```

```python
import functools
import math

import jax
import jax.numpy as jnp
import numpy as np
from jax import lax
from jax.experimental import pallas as pl
from jax.experimental.pallas import tpu as pltpu
from jax.sharding import PartitionSpec as P

LANES = 128


def fft_list(re, im):
    size = len(re)
    if size == 1:
        return re, im
    even_re, even_im = fft_list(re[0::2], im[0::2])
    odd_re, odd_im = fft_list(re[1::2], im[1::2])
    half = size // 2
    out_re, out_im = [None] * size, [None] * size
    for k in range(half):
        a, b = odd_re[k], odd_im[k]
        if k == 0:
            tr, ti = a, b
        elif 4 * k == size:
            tr, ti = b, -a
        elif 8 * k == size:
            h = math.sqrt(0.5)
            tr, ti = (a + b) * h, (b - a) * h
        elif 8 * k == 3 * size:
            h = math.sqrt(0.5)
            tr, ti = (b - a) * h, (a + b) * (-h)
        else:
            c, s = math.cos(2 * math.pi * k / size), math.sin(2 * math.pi * k / size)
            tr, ti = a * c + b * s, b * c - a * s
        out_re[k], out_re[k + half] = even_re[k] + tr, even_re[k] - tr
        out_im[k], out_im[k + half] = even_im[k] + ti, even_im[k] - ti
    return out_re, out_im


def transform_unit(radix, rows, frames, n, load, store, taps_ref, twr_ref, twi_ref, th_ref, tl_ref, mid_ref, y_ref):
    taps = taps_ref.shape[0]
    lags = min(taps, frames)
    sub = radix // 4
    gates = [jnp.where(n >= lag, 1.0, 0.0).astype(jnp.float32) for lag in range(lags)]
    index = [jnp.maximum(n - lag, 0) for lag in range(lags)]
    for a in range(4):
        tile_re, tile_im = [], []
        for j in range(sub):
            c1 = a + 4 * j
            cols = slice(c1 * LANES, (c1 + 1) * LANES)
            acc_re = acc_im = None
            for lag in range(lags):
                tap = taps_ref[taps - 1 - lag : taps - lag, cols]
                if lag:
                    tap = tap * gates[lag]
                pr = load(0, index[lag], cols).astype(jnp.float32) * tap
                pi = load(1, index[lag], cols).astype(jnp.float32) * tap
                acc_re = pr if acc_re is None else acc_re + pr
                acc_im = pi if acc_im is None else acc_im + pi
            tile_re.append(acc_re)
            tile_im.append(acc_im)
        out_re, out_im = fft_list(tile_re, tile_im)
        for q in range(sub):
            if a * q:
                c = math.cos(2 * math.pi * a * q / radix)
                s = math.sin(2 * math.pi * a * q / radix)
                mid_ref[0, a * sub + q] = out_re[q] * c + out_im[q] * s
                mid_ref[1, a * sub + q] = out_im[q] * c - out_re[q] * s
            else:
                mid_ref[0, a * sub + q] = out_re[q]
                mid_ref[1, a * sub + q] = out_im[q]
    for q in range(sub):
        out_re, out_im = fft_list(
            [mid_ref[0, a * sub + q] for a in range(4)], [mid_ref[1, a * sub + q] for a in range(4)]
        )
        for r in range(4):
            k1 = q + sub * r
            c = twr_ref[k1 : k1 + 1, :]
            s = twi_ref[k1 : k1 + 1, :]
            y_ref[k1 * rows : (k1 + 1) * rows, 0:LANES] = out_re[r] * c + out_im[r] * s
            y_ref[k1 * rows : (k1 + 1) * rows, LANES : 2 * LANES] = out_im[r] * c - out_re[r] * s
    y = y_ref[...]
    high = y.astype(jnp.bfloat16)
    low = (y - high.astype(jnp.float32)).astype(jnp.bfloat16)
    out = (
        jnp.dot(high, th_ref[...], preferred_element_type=jnp.float32)
        + jnp.dot(low, th_ref[...], preferred_element_type=jnp.float32)
        + jnp.dot(high, tl_ref[...], preferred_element_type=jnp.float32)
    ).astype(jnp.bfloat16)
    for k1 in range(radix):
        for p in range(2):
            store(k1, p, out[k1 * rows : (k1 + 1) * rows, p * LANES : (p + 1) * LANES])


def spectra_kernel(radix, groups, rows, x_ref, taps_ref, twr_ref, twi_ref, th_ref, tl_ref, o_ref, mid_ref, y_ref):
    frames = x_ref.shape[1]
    blocks = x_ref.shape[2] // rows
    per_group = radix // groups

    def unit(step, carry):
        n = step // blocks
        start = step % blocks * rows
        if rows % 16 == 0:
            start = pl.multiple_of(start, rows)

        def load(p, frame, cols):
            return x_ref[p, frame, pl.ds(start, rows), cols]

        def store(k1, p, value):
            kk = k1 % per_group
            o_ref[n * groups + k1 // per_group, p, pl.ds(start, rows), kk * LANES : (kk + 1) * LANES] = value

        transform_unit(
            radix, rows, frames, n, load, store, taps_ref, twr_ref, twi_ref, th_ref, tl_ref, mid_ref, y_ref
        )
        return carry

    lax.fori_loop(0, frames * blocks, unit, 0)


def tables(channels):
    radix = channels // LANES
    k1 = np.arange(radix)[:, None]
    c2 = np.arange(LANES)
    turn = 2.0 * np.pi * (k1 * c2[None, :]) / channels
    twr, twi = np.cos(turn).astype(np.float32), np.sin(turn).astype(np.float32)
    angle = 2.0 * np.pi * ((c2[:, None] * c2[None, :]) % LANES) / LANES
    cos, sin = np.cos(angle), np.sin(angle)
    table = (np.block([[cos, -sin], [sin, cos]]) / math.sqrt(channels)).astype(np.float32)
    table_high = table.astype(jnp.bfloat16)
    table_low = (table - table_high.astype(np.float32)).astype(jnp.bfloat16)
    return twr, twi, table_high, table_low


def make_spectra(x, filter_taps, groups):
    _, frames, inputs, channels = x.shape
    radix = channels // LANES
    rows = math.gcd(16, inputs)
    return pl.pallas_call(
        functools.partial(spectra_kernel, radix, groups, rows),
        out_shape=jax.ShapeDtypeStruct(
            (frames * groups, 2, inputs, channels // groups), jnp.bfloat16
        ),
        in_specs=[pl.BlockSpec(memory_space=pltpu.VMEM)] * 6,
        out_specs=pl.BlockSpec(memory_space=pltpu.VMEM),
        scratch_shapes=[
            pltpu.VMEM((2, radix, rows, LANES), jnp.float32),
            pltpu.VMEM((radix * rows, 2 * LANES), jnp.float32),
        ],
    )(x, filter_taps, *tables(channels))


def beam_kernel(scale, x_ref, w_ref, o_ref):
    groups, _, rows, width = x_ref.shape
    x_re = x_ref[:, 0].reshape(groups * rows, width)
    x_im = x_ref[:, 1].reshape(groups * rows, width)

    def block(step, carry):
        size = o_ref.shape[0] // 4
        start = pl.multiple_of(step * size, size)
        w_re = w_ref[0, pl.ds(start, size), :]
        w_im = w_ref[1, pl.ds(start, size), :]
        beam_re = jnp.dot(w_re, x_re, preferred_element_type=jnp.float32) - jnp.dot(
            w_im, x_im, preferred_element_type=jnp.float32
        )
        beam_im = jnp.dot(w_re, x_im, preferred_element_type=jnp.float32) + jnp.dot(
            w_im, x_re, preferred_element_type=jnp.float32
        )
        power = (beam_re * beam_re + beam_im * beam_im) * scale
        o_ref[pl.ds(start, size), :] = power.astype(jnp.bfloat16)
        return carry

    lax.fori_loop(0, 4, block, 0)


def make_power(spectra, weights):
    inputs_all = weights.shape[2]
    if spectra.shape[2] % 16:
        spectra = spectra.transpose(1, 0, 2, 3).reshape(1, 2, inputs_all, spectra.shape[3])
    return pl.pallas_call(
        functools.partial(beam_kernel, 1.0 / inputs_all),
        out_shape=jax.ShapeDtypeStruct((weights.shape[1], spectra.shape[3]), jnp.bfloat16),
        in_specs=[pl.BlockSpec(memory_space=pltpu.VMEM)] * 2,
        out_specs=pl.BlockSpec(memory_space=pltpu.VMEM),
    )(spectra, weights)


def local_weights(beam_weights, station_map, station_flags, tm_size, stn_size):
    inputs_all = beam_weights.shape[2]
    few = inputs_all // (tm_size * stn_size)
    column = jnp.arange(inputs_all, dtype=jnp.int32)
    source, inner = column // few, column % few
    slot_input = (source % stn_size) * (few * tm_size) + (source // stn_size) * few + inner
    flag = station_flags[station_map]
    wanted = (2 * station_map[slot_input // 2] + slot_input % 2).astype(jnp.int32)
    keep = flag[slot_input // 2]
    pick = (jnp.arange(inputs_all, dtype=jnp.int32)[:, None] == wanted[None, :]) & (keep[None, :] != 0)
    low = (beam_weights.astype(jnp.float32) * (1.0 / 32768.0)).astype(jnp.bfloat16)
    return jnp.dot(
        low.reshape(-1, inputs_all), pick.astype(jnp.bfloat16), preferred_element_type=jnp.float32
    ).astype(jnp.bfloat16).reshape(low.shape)


def fused_kernel(
    tm, stn, radix, scale,
    v_ref, w_ref, map_ref, flag_ref, taps_ref, twr_ref, twi_ref, th_ref, tl_ref,
    o_ref,
    xbuf, sbuf, rbuf, wbuf, acc, pbuf, qbuf, mid_ref, y_ref,
    v_send, v_recv, up_send, up_recv, down_send, down_recv, side_send, side_recv,
    s_send, s_recv, p_send, p_recv, o_sem,
):
    halves, rows = xbuf.shape[0], xbuf.shape[3]
    chips = stn // 2
    per_group = radix // stn
    me_t, me_s = lax.axis_index("tm"), lax.axis_index("stn")
    z, core = me_s // 2, me_s % 2
    me = me_t * stn + me_s
    width = rbuf.shape[4]

    def remote(src, dst, send, recv, t, s):
        return pltpu.make_async_remote_copy(
            src_ref=src, dst_ref=dst, send_sem=send, recv_sem=recv,
            device_id=(t, s), device_id_type=pl.DeviceIdType.MESH,
        )

    def settle(ref, sem):
        pltpu.make_async_copy(ref, ref, sem).wait()

    barrier = pltpu.get_barrier_semaphore()

    def greet(d, carry):
        other = lax.rem(me + d, tm * stn)
        pl.semaphore_signal(
            barrier, inc=1, device_id=(other // stn, other % stn), device_id_type=pl.DeviceIdType.MESH
        )
        return carry

    lax.fori_loop(1, tm * stn, greet, 0)
    beams, inputs_all = w_ref.shape[1], w_ref.shape[2]
    stations = map_ref.shape[1]
    few = halves * rows
    number = jnp.broadcast_to(map_ref[...], (8, stations))
    flags = jnp.broadcast_to(flag_ref[...], (8, stations))
    row = lax.broadcasted_iota(jnp.int32, (8, stations), 0)
    facts = jnp.where(row == 0, number >> 4, jnp.where(row == 1, number & 15, flags))
    facts = facts.astype(jnp.float32).astype(jnp.bfloat16)
    step = min(256, inputs_all)

    def look_up(slot):
        slots = lax.broadcasted_iota(jnp.int32, (stations, step), 0)
        pick = jnp.where(slots == slot, 1.0, 0.0).astype(jnp.bfloat16)
        return jnp.dot(facts, pick, preferred_element_type=jnp.float32)

    low = []
    for first in range(0, inputs_all, step):
        column = first + lax.broadcasted_iota(jnp.int32, (1, step), 1)
        keep = look_up(column >> 1)[2:3] * (1.0 / 32768.0)
        low.append((w_ref[:, :, first : first + step].astype(jnp.float32) * keep[None]).astype(jnp.bfloat16))
    low = jnp.concatenate(low, axis=2).reshape(2 * beams, inputs_all)
    for first in range(0, inputs_all, step):
        column = first + lax.broadcasted_iota(jnp.int32, (1, step), 1)
        part = inputs_all // halves
        h, rest = lax.div(column, part), lax.rem(column, part)
        source, inner = lax.div(rest, rows), lax.rem(rest, rows)
        ours = lax.rem(source, stn) * (few * tm) + lax.div(source, stn) * few + h * rows + inner
        found = look_up(ours >> 1)
        wanted = (found[0:1] * 32.0 + found[1:2] * 2.0).astype(jnp.int32) + (ours & 1)
        station = lax.broadcasted_iota(jnp.int32, (inputs_all, step), 0)
        pick = jnp.where(station == wanted, 1.0, 0.0).astype(jnp.bfloat16)
        wbuf[me_s, :, first : first + step] = jnp.dot(
            low, pick, preferred_element_type=jnp.float32
        ).astype(jnp.bfloat16)

    pl.semaphore_wait(barrier, tm * stn - 1)

    def to_side(block):
        slot = 2 * block + core
        remote(wbuf.at[slot], wbuf.at[slot], side_send.at[block], side_recv.at[block], me_t, 2 * z + 1 - core).start()

    def chain_send(r):
        @pl.when((z >= r) & (z < chips - 1))
        def _():
            slot = 2 * (z - r) + core
            remote(wbuf.at[slot], wbuf.at[slot], up_send.at[r], up_recv.at[r], me_t, me_s + 2).start()

        @pl.when((z + r <= chips - 1) & (z > 0))
        def _():
            slot = 2 * (z + r) + core
            remote(wbuf.at[slot], wbuf.at[slot], down_send.at[r], down_recv.at[r], me_t, me_s - 2).start()

    def chain_recv(r):
        @pl.when(z - 1 - r >= 0)
        def _():
            settle(wbuf.at[0], up_recv.at[r])
            to_side(z - 1 - r)

        @pl.when(z + 1 + r <= chips - 1)
        def _():
            settle(wbuf.at[0], down_recv.at[r])
            to_side(z + 1 + r)

    chain_send(0)
    to_side(z)

    for h in range(halves):
        for d in range(1, tm):
            t = lax.rem(me_t + d, tm)
            remote(
                v_ref.at[:, t, h * rows : (h + 1) * rows], xbuf.at[h, :, me_t],
                v_send.at[h], v_recv.at[h], t, me_s,
            ).start()
        pltpu.make_async_copy(
            v_ref.at[:, me_t, h * rows : (h + 1) * rows], xbuf.at[h, :, me_t], v_recv.at[h]
        ).start()

    for r in range(1, chips - 1):
        if r < chips - 2:
            chain_recv(r - 1)
            chain_send(r)

    for h in range(halves):
        settle(xbuf.at[h], v_recv.at[h])

        def frame(j, carry):
            n = lax.rem(me_t + j, tm)

            def load(p, index, cols):
                return xbuf[h, p, index, :, cols]

            def store(k1, p, value):
                kk = k1 % per_group
                sbuf[h, n * stn + k1 // per_group, p, :, kk * LANES : (kk + 1) * LANES] = value

            transform_unit(
                radix, rows, tm, n, load, store, taps_ref, twr_ref, twi_ref, th_ref, tl_ref, mid_ref, y_ref
            )

            def send(e, inner):
                s = lax.rem(me_s + e, stn)
                remote(
                    sbuf.at[h, n * stn + s], rbuf.at[h, me], s_send.at[h], s_recv.at[h], n, s
                ).start()
                return inner

            lax.fori_loop(1, stn, send, 0)

            @pl.when(j > 0)
            def _():
                send(0, 0)

            @pl.when(j == 0)
            def _():
                pltpu.make_async_copy(sbuf.at[h, me], rbuf.at[h, me], s_recv.at[h]).start()

            return carry

        lax.fori_loop(0, tm, frame, 0)
        if h == 0:
            if chips > 2:
                chain_recv(chips - 3)
                chain_send(chips - 2)
    if chips > 1:
        chain_recv(chips - 2)

    for block in range(chips):
        settle(wbuf.at[0], side_recv.at[block])

    def beams_of(h, pair):
        cols = slice(h * inputs_all // halves, (h + 1) * inputs_all // halves)
        w = wbuf[pl.ds(2 * pair, 2), :, cols].reshape(4 * beams, inputs_all // halves)
        x_re = rbuf[h, :, 0].reshape(inputs_all // halves, width)
        x_im = rbuf[h, :, 1].reshape(inputs_all // halves, width)
        by_re = jnp.dot(w, x_re, preferred_element_type=jnp.float32).reshape(2, 2, beams, width)
        by_im = jnp.dot(w, x_im, preferred_element_type=jnp.float32).reshape(2, 2, beams, width)
        return by_re[:, 0] - by_im[:, 1], by_im[:, 0] + by_re[:, 1]

    for h in range(halves - 1):
        settle(rbuf.at[h], s_recv.at[h])

        def collect(pair, carry):
            beam_re, beam_im = beams_of(h, pair)
            two = pl.ds(2 * pair, 2)
            if h:
                beam_re, beam_im = beam_re + acc[0, two], beam_im + acc[1, two]
            acc[0, two] = beam_re
            acc[1, two] = beam_im
            return carry

        lax.fori_loop(0, chips, collect, 0)

    settle(rbuf.at[halves - 1], s_recv.at[halves - 1])

    def finish(i, carry):
        pair = lax.rem(z + 1 + i, chips)
        beam_re, beam_im = beams_of(halves - 1, pair)
        two = pl.ds(2 * pair, 2)
        if halves > 1:
            beam_re, beam_im = beam_re + acc[0, two], beam_im + acc[1, two]
        qbuf[two] = ((beam_re * beam_re + beam_im * beam_im) * scale).astype(jnp.bfloat16)
        other = 2 * pair + 1 - core
        same = 2 * pair + core
        remote(qbuf.at[other], pbuf.at[me_s], p_send, p_recv, me_t, other).start()

        @pl.when(i < chips - 1)
        def _():
            remote(qbuf.at[same], pbuf.at[me_s], p_send, p_recv, me_t, same).start()

        @pl.when(i == chips - 1)
        def _():
            pltpu.make_async_copy(qbuf.at[me_s], pbuf.at[me_s], p_recv).start()

        return carry

    lax.fori_loop(0, chips, finish, 0)

    for h in range(halves):
        settle(xbuf.at[h, :, 0 : tm - 1], v_send.at[h])
        settle(sbuf.at[h, 0 : tm * stn - 1], s_send.at[h])
    for block in range(chips):
        settle(wbuf.at[0], side_send.at[block])
    for r in range(chips - 1):
        @pl.when((z >= r) & (z < chips - 1))
        def _():
            settle(wbuf.at[0], up_send.at[r])

        @pl.when((z + r <= chips - 1) & (z > 0))
        def _():
            settle(wbuf.at[0], down_send.at[r])
    settle(qbuf.at[0 : stn - 1], p_send)
    settle(pbuf, p_recv)
    out = pltpu.make_async_copy(pbuf, o_ref, o_sem)
    out.start()
    out.wait()


def fused(tm, stn, voltages, filter_taps, beam_weights, station_map, station_flags):
    channels = filter_taps.shape[1]
    radix = channels // LANES
    few = voltages.shape[1] // tm
    halves = 2
    rows = few // halves
    width = channels // stn
    beams, inputs_all = beam_weights.shape[1], beam_weights.shape[2]
    chips = stn // 2
    stations = station_map.shape[0]
    dma = pltpu.SemaphoreType.DMA
    vmem = pl.BlockSpec(memory_space=pltpu.VMEM)
    hbm = pl.BlockSpec(memory_space=pl.ANY)
    low = jnp.bfloat16
    return pl.pallas_call(
        functools.partial(fused_kernel, tm, stn, radix, 1.0 / inputs_all),
        out_shape=jax.ShapeDtypeStruct((stn, beams, width), low),
        in_specs=[hbm] + [vmem] * 8,
        out_specs=hbm,
        scratch_shapes=[
            pltpu.VMEM((halves, 2, tm, rows, channels), low),
            pltpu.VMEM((halves, tm * stn, 2, rows, width), low),
            pltpu.VMEM((halves, tm * stn, 2, rows, width), low),
            pltpu.VMEM((stn, 2 * beams, inputs_all), low),
            pltpu.VMEM((2, stn, beams, width), jnp.float32),
            pltpu.VMEM((stn, beams, width), low),
            pltpu.VMEM((stn, beams, width), low),
            pltpu.VMEM((2, radix, rows, LANES), jnp.float32),
            pltpu.VMEM((radix * rows, 2 * LANES), jnp.float32),
            dma((halves,)), dma((halves,)),
            dma((chips,)), dma((chips,)), dma((chips,)), dma((chips,)), dma((chips,)), dma((chips,)),
            dma((halves,)), dma((halves,)), dma, dma, dma,
        ],
        compiler_params=pltpu.CompilerParams(collective_id=0, has_side_effects=True),
    )(
        voltages.reshape(2, tm, few, channels), beam_weights, station_map.reshape(1, stations),
        station_flags.reshape(1, stations), filter_taps, *tables(channels),
    )


def order_kernel(p_ref, o_ref, rows_ref):
    stn, beams, width = p_ref.shape
    radix = o_ref.shape[1]
    per_group = width // LANES
    cuts = LANES // radix
    for source in range(stn):
        for kk in range(per_group):
            rows_ref[pl.ds(source * per_group + kk, beams, stride=radix), :] = p_ref[
                source, :, kk * LANES : (kk + 1) * LANES
            ].astype(jnp.float32)
    row = lax.broadcasted_iota(jnp.int32, (LANES, LANES), 0)
    lane = lax.broadcasted_iota(jnp.int32, (LANES, LANES), 1)
    chosen = lax.rem(row, radix) * cuts + lax.div(row, radix)
    pick = jnp.where(lane == chosen, 1.0, 0.0).astype(jnp.bfloat16)
    turned = lax.dot_general(
        pick, rows_ref[...].astype(jnp.bfloat16), (((1,), (1,)), ((), ())), preferred_element_type=jnp.float32
    )
    place = lax.div(lax.broadcasted_iota(jnp.int32, (radix, LANES), 1), radix)
    for tile in range(beams * radix // LANES):
        parts = [turned[j * radix : (j + 1) * radix, tile * LANES : (tile + 1) * LANES] for j in range(cuts)]
        for bb in range(cuts):
            out = None
            for j in range(cuts):
                shift = (j - bb) % cuts * radix
                moved = pltpu.roll(parts[j], shift, 1) if shift else parts[j]
                out = moved if out is None else jnp.where(place == j, moved, out)
            o_ref[tile * cuts + bb] = out


def put_in_order(mine, radix):
    stn, beams, _ = mine.shape
    return pl.pallas_call(
        order_kernel,
        out_shape=jax.ShapeDtypeStruct((beams, radix, LANES), jnp.float32),
        in_specs=[pl.BlockSpec(memory_space=pltpu.VMEM)],
        out_specs=pl.BlockSpec(memory_space=pltpu.VMEM),
        scratch_shapes=[pltpu.VMEM((beams * radix, LANES), jnp.float32)],
    )(mine)


def on_device(tm_size, stn_size, voltages, filter_taps, beam_weights, station_map, station_flags):
    channels = filter_taps.shape[1]
    few = voltages.shape[1] // tm_size
    if few % 32 == 0 and stn_size % 2 == 0:
        mine = fused(tm_size, stn_size, voltages, filter_taps, beam_weights, station_map, station_flags)
        return put_in_order(mine, channels // LANES).reshape(mine.shape[1], 1, channels)
    else:
        weights = local_weights(beam_weights, station_map, station_flags, tm_size, stn_size)
        weight_all = lax.all_gather(weights, "stn", axis=1, tiled=True)
        frames = voltages.reshape(2, tm_size, few, channels)
        frames = lax.all_to_all(frames, "tm", split_axis=1, concat_axis=1, tiled=True)
        spectra = make_spectra(frames, filter_taps, stn_size)
        turned = lax.all_to_all(spectra, ("tm", "stn"), split_axis=0, concat_axis=0, tiled=True)
        power = make_power(turned, weight_all)
        beams = power.shape[0] // stn_size
        mine = lax.all_to_all(
            power.reshape(stn_size, beams, -1), "stn", split_axis=0, concat_axis=0, tiled=True
        )
    radix = channels // LANES
    mine = mine.reshape(stn_size, beams, radix // stn_size, LANES).astype(jnp.float32)
    return mine.transpose(1, 3, 0, 2).reshape(beams, 1, channels)


def solution(mesh):
    placed = (P(None, "stn", "tm"), P(), P(None, "stn", None), P(), P())
    body = functools.partial(on_device, mesh.shape["tm"], mesh.shape["stn"])
    return jax.shard_map(
        body, mesh=mesh, in_specs=placed, out_specs=P("stn", "tm", None), check_vma=False
    )
```

```python
import functools
import math

import jax
import jax.numpy as jnp
import numpy as np
from jax import lax
from jax.experimental import pallas as pl
from jax.experimental.pallas import tpu as pltpu
from jax.sharding import PartitionSpec as P

LANES = 128


def fft_list(re, im):
    size = len(re)
    if size == 1:
        return re, im
    even_re, even_im = fft_list(re[0::2], im[0::2])
    odd_re, odd_im = fft_list(re[1::2], im[1::2])
    half = size // 2
    out_re, out_im = [None] * size, [None] * size
    for k in range(half):
        a, b = odd_re[k], odd_im[k]
        if k == 0:
            tr, ti = a, b
        elif 4 * k == size:
            tr, ti = b, -a
        elif 8 * k == size:
            h = math.sqrt(0.5)
            tr, ti = (a + b) * h, (b - a) * h
        elif 8 * k == 3 * size:
            h = math.sqrt(0.5)
            tr, ti = (b - a) * h, (a + b) * (-h)
        else:
            c, s = math.cos(2 * math.pi * k / size), math.sin(2 * math.pi * k / size)
            tr, ti = a * c + b * s, b * c - a * s
        out_re[k], out_re[k + half] = even_re[k] + tr, even_re[k] - tr
        out_im[k], out_im[k + half] = even_im[k] + ti, even_im[k] - ti
    return out_re, out_im


def transform_unit(radix, rows, frames, n, load, store, taps_ref, twr_ref, twi_ref, th_ref, tl_ref, mid_ref, y_ref):
    taps = taps_ref.shape[0]
    lags = min(taps, frames)
    sub = radix // 4
    gates = [jnp.where(n >= lag, 1.0, 0.0).astype(jnp.float32) for lag in range(lags)]
    index = [jnp.maximum(n - lag, 0) for lag in range(lags)]
    for a in range(4):
        tile_re, tile_im = [], []
        for j in range(sub):
            c1 = a + 4 * j
            cols = slice(c1 * LANES, (c1 + 1) * LANES)
            acc_re = acc_im = None
            for lag in range(lags):
                tap = taps_ref[taps - 1 - lag : taps - lag, cols]
                if lag:
                    tap = tap * gates[lag]
                pr = load(0, index[lag], cols).astype(jnp.float32) * tap
                pi = load(1, index[lag], cols).astype(jnp.float32) * tap
                acc_re = pr if acc_re is None else acc_re + pr
                acc_im = pi if acc_im is None else acc_im + pi
            tile_re.append(acc_re)
            tile_im.append(acc_im)
        out_re, out_im = fft_list(tile_re, tile_im)
        for q in range(sub):
            if a * q:
                c = math.cos(2 * math.pi * a * q / radix)
                s = math.sin(2 * math.pi * a * q / radix)
                mid_ref[0, a * sub + q] = out_re[q] * c + out_im[q] * s
                mid_ref[1, a * sub + q] = out_im[q] * c - out_re[q] * s
            else:
                mid_ref[0, a * sub + q] = out_re[q]
                mid_ref[1, a * sub + q] = out_im[q]
    for q in range(sub):
        out_re, out_im = fft_list(
            [mid_ref[0, a * sub + q] for a in range(4)], [mid_ref[1, a * sub + q] for a in range(4)]
        )
        for r in range(4):
            k1 = q + sub * r
            c = twr_ref[k1 : k1 + 1, :]
            s = twi_ref[k1 : k1 + 1, :]
            y_ref[k1 * rows : (k1 + 1) * rows, 0:LANES] = out_re[r] * c + out_im[r] * s
            y_ref[k1 * rows : (k1 + 1) * rows, LANES : 2 * LANES] = out_im[r] * c - out_re[r] * s
    y = y_ref[...]
    high = y.astype(jnp.bfloat16)
    low = (y - high.astype(jnp.float32)).astype(jnp.bfloat16)
    out = (
        jnp.dot(high, th_ref[...], preferred_element_type=jnp.float32)
        + jnp.dot(low, th_ref[...], preferred_element_type=jnp.float32)
        + jnp.dot(high, tl_ref[...], preferred_element_type=jnp.float32)
    ).astype(jnp.bfloat16)
    for k1 in range(radix):
        for p in range(2):
            store(k1, p, out[k1 * rows : (k1 + 1) * rows, p * LANES : (p + 1) * LANES])


def spectra_kernel(radix, groups, rows, x_ref, taps_ref, twr_ref, twi_ref, th_ref, tl_ref, o_ref, mid_ref, y_ref):
    frames = x_ref.shape[1]
    blocks = x_ref.shape[2] // rows
    per_group = radix // groups

    def unit(step, carry):
        n = step // blocks
        start = step % blocks * rows
        if rows % 16 == 0:
            start = pl.multiple_of(start, rows)

        def load(p, frame, cols):
            return x_ref[p, frame, pl.ds(start, rows), cols]

        def store(k1, p, value):
            kk = k1 % per_group
            o_ref[n * groups + k1 // per_group, p, pl.ds(start, rows), kk * LANES : (kk + 1) * LANES] = value

        transform_unit(
            radix, rows, frames, n, load, store, taps_ref, twr_ref, twi_ref, th_ref, tl_ref, mid_ref, y_ref
        )
        return carry

    lax.fori_loop(0, frames * blocks, unit, 0)


def tables(channels):
    radix = channels // LANES
    k1 = np.arange(radix)[:, None]
    c2 = np.arange(LANES)
    turn = 2.0 * np.pi * (k1 * c2[None, :]) / channels
    twr, twi = np.cos(turn).astype(np.float32), np.sin(turn).astype(np.float32)
    angle = 2.0 * np.pi * ((c2[:, None] * c2[None, :]) % LANES) / LANES
    cos, sin = np.cos(angle), np.sin(angle)
    table = (np.block([[cos, -sin], [sin, cos]]) / math.sqrt(channels)).astype(np.float32)
    table_high = table.astype(jnp.bfloat16)
    table_low = (table - table_high.astype(np.float32)).astype(jnp.bfloat16)
    return twr, twi, table_high, table_low


def make_spectra(x, filter_taps, groups):
    _, frames, inputs, channels = x.shape
    radix = channels // LANES
    rows = math.gcd(16, inputs)
    return pl.pallas_call(
        functools.partial(spectra_kernel, radix, groups, rows),
        out_shape=jax.ShapeDtypeStruct(
            (frames * groups, 2, inputs, channels // groups), jnp.bfloat16
        ),
        in_specs=[pl.BlockSpec(memory_space=pltpu.VMEM)] * 6,
        out_specs=pl.BlockSpec(memory_space=pltpu.VMEM),
        scratch_shapes=[
            pltpu.VMEM((2, radix, rows, LANES), jnp.float32),
            pltpu.VMEM((radix * rows, 2 * LANES), jnp.float32),
        ],
    )(x, filter_taps, *tables(channels))


def beam_kernel(scale, x_ref, w_ref, o_ref):
    groups, _, rows, width = x_ref.shape
    x_re = x_ref[:, 0].reshape(groups * rows, width)
    x_im = x_ref[:, 1].reshape(groups * rows, width)

    def block(step, carry):
        size = o_ref.shape[0] // 4
        start = pl.multiple_of(step * size, size)
        w_re = w_ref[0, pl.ds(start, size), :]
        w_im = w_ref[1, pl.ds(start, size), :]
        beam_re = jnp.dot(w_re, x_re, preferred_element_type=jnp.float32) - jnp.dot(
            w_im, x_im, preferred_element_type=jnp.float32
        )
        beam_im = jnp.dot(w_re, x_im, preferred_element_type=jnp.float32) + jnp.dot(
            w_im, x_re, preferred_element_type=jnp.float32
        )
        power = (beam_re * beam_re + beam_im * beam_im) * scale
        o_ref[pl.ds(start, size), :] = power.astype(jnp.bfloat16)
        return carry

    lax.fori_loop(0, 4, block, 0)


def make_power(spectra, weights):
    inputs_all = weights.shape[2]
    if spectra.shape[2] % 16:
        spectra = spectra.transpose(1, 0, 2, 3).reshape(1, 2, inputs_all, spectra.shape[3])
    return pl.pallas_call(
        functools.partial(beam_kernel, 1.0 / inputs_all),
        out_shape=jax.ShapeDtypeStruct((weights.shape[1], spectra.shape[3]), jnp.bfloat16),
        in_specs=[pl.BlockSpec(memory_space=pltpu.VMEM)] * 2,
        out_specs=pl.BlockSpec(memory_space=pltpu.VMEM),
    )(spectra, weights)


def local_weights(beam_weights, station_map, station_flags, tm_size, stn_size):
    inputs_all = beam_weights.shape[2]
    few = inputs_all // (tm_size * stn_size)
    column = jnp.arange(inputs_all, dtype=jnp.int32)
    source, inner = column // few, column % few
    slot_input = (source % stn_size) * (few * tm_size) + (source // stn_size) * few + inner
    flag = station_flags[station_map]
    wanted = (2 * station_map[slot_input // 2] + slot_input % 2).astype(jnp.int32)
    keep = flag[slot_input // 2]
    pick = (jnp.arange(inputs_all, dtype=jnp.int32)[:, None] == wanted[None, :]) & (keep[None, :] != 0)
    low = (beam_weights.astype(jnp.float32) * (1.0 / 32768.0)).astype(jnp.bfloat16)
    return jnp.dot(
        low.reshape(-1, inputs_all), pick.astype(jnp.bfloat16), preferred_element_type=jnp.float32
    ).astype(jnp.bfloat16).reshape(low.shape)


def fused_kernel(
    tm, stn, radix, scale,
    v_ref, w_ref, map_ref, flag_ref, taps_ref, twr_ref, twi_ref, th_ref, tl_ref,
    o_ref,
    xbuf, sbuf, rbuf, wbuf, acc, pbuf, qbuf, mid_ref, y_ref,
    v_send, v_recv, up_send, up_recv, down_send, down_recv, side_send, side_recv,
    s_send, s_recv, p_send, p_recv, o_sem,
):
    halves, rows = xbuf.shape[0], xbuf.shape[3]
    chips = stn // 2
    per_group = radix // stn
    me_t, me_s = lax.axis_index("tm"), lax.axis_index("stn")
    z, core = me_s // 2, me_s % 2
    me = me_t * stn + me_s
    width = rbuf.shape[4]

    def remote(src, dst, send, recv, t, s):
        return pltpu.make_async_remote_copy(
            src_ref=src, dst_ref=dst, send_sem=send, recv_sem=recv,
            device_id=(t, s), device_id_type=pl.DeviceIdType.MESH,
        )

    def settle(ref, sem):
        pltpu.make_async_copy(ref, ref, sem).wait()

    barrier = pltpu.get_barrier_semaphore()

    def greet(d, carry):
        other = lax.rem(me + d, tm * stn)
        pl.semaphore_signal(
            barrier, inc=1, device_id=(other // stn, other % stn), device_id_type=pl.DeviceIdType.MESH
        )
        return carry

    lax.fori_loop(1, tm * stn, greet, 0)
    beams, inputs_all = w_ref.shape[1], w_ref.shape[2]
    stations = map_ref.shape[1]
    few = halves * rows
    number = jnp.broadcast_to(map_ref[...], (8, stations))
    flags = jnp.broadcast_to(flag_ref[...], (8, stations))
    row = lax.broadcasted_iota(jnp.int32, (8, stations), 0)
    facts = jnp.where(row == 0, number >> 4, jnp.where(row == 1, number & 15, flags))
    facts = facts.astype(jnp.float32).astype(jnp.bfloat16)
    step = min(256, inputs_all)

    def look_up(slot):
        slots = lax.broadcasted_iota(jnp.int32, (stations, step), 0)
        pick = jnp.where(slots == slot, 1.0, 0.0).astype(jnp.bfloat16)
        return jnp.dot(facts, pick, preferred_element_type=jnp.float32)

    low = []
    for first in range(0, inputs_all, step):
        column = first + lax.broadcasted_iota(jnp.int32, (1, step), 1)
        keep = look_up(column >> 1)[2:3] * (1.0 / 32768.0)
        low.append((w_ref[:, :, first : first + step].astype(jnp.float32) * keep[None]).astype(jnp.bfloat16))
    low = jnp.concatenate(low, axis=2).reshape(2 * beams, inputs_all)
    for first in range(0, inputs_all, step):
        column = first + lax.broadcasted_iota(jnp.int32, (1, step), 1)
        part = inputs_all // halves
        h, rest = lax.div(column, part), lax.rem(column, part)
        source, inner = lax.div(rest, rows), lax.rem(rest, rows)
        ours = lax.rem(source, stn) * (few * tm) + lax.div(source, stn) * few + h * rows + inner
        found = look_up(ours >> 1)
        wanted = (found[0:1] * 32.0 + found[1:2] * 2.0).astype(jnp.int32) + (ours & 1)
        station = lax.broadcasted_iota(jnp.int32, (inputs_all, step), 0)
        pick = jnp.where(station == wanted, 1.0, 0.0).astype(jnp.bfloat16)
        wbuf[me_s, :, first : first + step] = jnp.dot(
            low, pick, preferred_element_type=jnp.float32
        ).astype(jnp.bfloat16)

    pl.semaphore_wait(barrier, tm * stn - 1)

    def to_side(block):
        slot = 2 * block + core
        remote(wbuf.at[slot], wbuf.at[slot], side_send.at[block], side_recv.at[block], me_t, 2 * z + 1 - core).start()

    def chain_send(r):
        @pl.when((z >= r) & (z < chips - 1))
        def _():
            slot = 2 * (z - r) + core
            remote(wbuf.at[slot], wbuf.at[slot], up_send.at[r], up_recv.at[r], me_t, me_s + 2).start()

        @pl.when((z + r <= chips - 1) & (z > 0))
        def _():
            slot = 2 * (z + r) + core
            remote(wbuf.at[slot], wbuf.at[slot], down_send.at[r], down_recv.at[r], me_t, me_s - 2).start()

    def chain_recv(r):
        @pl.when(z - 1 - r >= 0)
        def _():
            settle(wbuf.at[0], up_recv.at[r])
            to_side(z - 1 - r)

        @pl.when(z + 1 + r <= chips - 1)
        def _():
            settle(wbuf.at[0], down_recv.at[r])
            to_side(z + 1 + r)

    chain_send(0)
    to_side(z)

    for h in range(halves):
        for d in range(1, tm):
            t = lax.rem(me_t + d, tm)
            remote(
                v_ref.at[:, t, h * rows : (h + 1) * rows], xbuf.at[h, :, me_t],
                v_send.at[h], v_recv.at[h], t, me_s,
            ).start()
        pltpu.make_async_copy(
            v_ref.at[:, me_t, h * rows : (h + 1) * rows], xbuf.at[h, :, me_t], v_recv.at[h]
        ).start()

    for r in range(1, chips - 1):
        if r < chips - 2:
            chain_recv(r - 1)
            chain_send(r)

    for h in range(halves):
        settle(xbuf.at[h], v_recv.at[h])

        def frame(j, carry):
            n = lax.rem(me_t + j, tm)

            def load(p, index, cols):
                return xbuf[h, p, index, :, cols]

            def store(k1, p, value):
                kk = k1 % per_group
                sbuf[h, n * stn + k1 // per_group, p, :, kk * LANES : (kk + 1) * LANES] = value

            transform_unit(
                radix, rows, tm, n, load, store, taps_ref, twr_ref, twi_ref, th_ref, tl_ref, mid_ref, y_ref
            )

            def send(e, inner):
                s = lax.rem(me_s + e, stn)
                remote(
                    sbuf.at[h, n * stn + s], rbuf.at[h, me], s_send.at[h], s_recv.at[h], n, s
                ).start()
                return inner

            lax.fori_loop(1, stn, send, 0)

            @pl.when(j > 0)
            def _():
                send(0, 0)

            @pl.when(j == 0)
            def _():
                pltpu.make_async_copy(sbuf.at[h, me], rbuf.at[h, me], s_recv.at[h]).start()

            return carry

        lax.fori_loop(0, tm, frame, 0)
        if h == 0:
            if chips > 2:
                chain_recv(chips - 3)
                chain_send(chips - 2)
    if chips > 1:
        chain_recv(chips - 2)

    for block in range(chips):
        settle(wbuf.at[0], side_recv.at[block])

    def beams_of(h, pair):
        cols = slice(h * inputs_all // halves, (h + 1) * inputs_all // halves)
        w = wbuf[pl.ds(2 * pair, 2), :, cols].reshape(4 * beams, inputs_all // halves)
        x_re = rbuf[h, :, 0].reshape(inputs_all // halves, width)
        x_im = rbuf[h, :, 1].reshape(inputs_all // halves, width)
        by_re = jnp.dot(w, x_re, preferred_element_type=jnp.float32).reshape(2, 2, beams, width)
        by_im = jnp.dot(w, x_im, preferred_element_type=jnp.float32).reshape(2, 2, beams, width)
        return by_re[:, 0] - by_im[:, 1], by_im[:, 0] + by_re[:, 1]

    for h in range(halves - 1):
        settle(rbuf.at[h], s_recv.at[h])

        def collect(pair, carry):
            beam_re, beam_im = beams_of(h, pair)
            two = pl.ds(2 * pair, 2)
            if h:
                beam_re, beam_im = beam_re + acc[0, two], beam_im + acc[1, two]
            acc[0, two] = beam_re
            acc[1, two] = beam_im
            return carry

        lax.fori_loop(0, chips, collect, 0)

    settle(rbuf.at[halves - 1], s_recv.at[halves - 1])

    def finish(i, carry):
        pair = lax.rem(z + 1 + i, chips)
        beam_re, beam_im = beams_of(halves - 1, pair)
        two = pl.ds(2 * pair, 2)
        if halves > 1:
            beam_re, beam_im = beam_re + acc[0, two], beam_im + acc[1, two]
        qbuf[two] = ((beam_re * beam_re + beam_im * beam_im) * scale).astype(jnp.bfloat16)
        other = 2 * pair + 1 - core
        same = 2 * pair + core
        remote(qbuf.at[other], pbuf.at[me_s], p_send, p_recv, me_t, other).start()

        @pl.when(i < chips - 1)
        def _():
            remote(qbuf.at[same], pbuf.at[me_s], p_send, p_recv, me_t, same).start()

        @pl.when(i == chips - 1)
        def _():
            pltpu.make_async_copy(qbuf.at[me_s], pbuf.at[me_s], p_recv).start()

        return carry

    lax.fori_loop(0, chips, finish, 0)

    for h in range(halves):
        settle(xbuf.at[h, :, 0 : tm - 1], v_send.at[h])
        settle(sbuf.at[h, 0 : tm * stn - 1], s_send.at[h])
    for block in range(chips):
        settle(wbuf.at[0], side_send.at[block])
    for r in range(chips - 1):
        @pl.when((z >= r) & (z < chips - 1))
        def _():
            settle(wbuf.at[0], up_send.at[r])

        @pl.when((z + r <= chips - 1) & (z > 0))
        def _():
            settle(wbuf.at[0], down_send.at[r])
    settle(qbuf.at[0 : stn - 1], p_send)
    settle(pbuf, p_recv)
    out = pltpu.make_async_copy(pbuf, o_ref, o_sem)
    out.start()
    out.wait()


def fused(tm, stn, voltages, filter_taps, beam_weights, station_map, station_flags):
    channels = filter_taps.shape[1]
    radix = channels // LANES
    few = voltages.shape[1] // tm
    halves = 4
    rows = few // halves
    width = channels // stn
    beams, inputs_all = beam_weights.shape[1], beam_weights.shape[2]
    chips = stn // 2
    stations = station_map.shape[0]
    dma = pltpu.SemaphoreType.DMA
    vmem = pl.BlockSpec(memory_space=pltpu.VMEM)
    hbm = pl.BlockSpec(memory_space=pl.ANY)
    low = jnp.bfloat16
    return pl.pallas_call(
        functools.partial(fused_kernel, tm, stn, radix, 1.0 / inputs_all),
        out_shape=jax.ShapeDtypeStruct((stn, beams, width), low),
        in_specs=[hbm] + [vmem] * 8,
        out_specs=hbm,
        scratch_shapes=[
            pltpu.VMEM((halves, 2, tm, rows, channels), low),
            pltpu.VMEM((halves, tm * stn, 2, rows, width), low),
            pltpu.VMEM((halves, tm * stn, 2, rows, width), low),
            pltpu.VMEM((stn, 2 * beams, inputs_all), low),
            pltpu.VMEM((2, stn, beams, width), jnp.float32),
            pltpu.VMEM((stn, beams, width), low),
            pltpu.VMEM((stn, beams, width), low),
            pltpu.VMEM((2, radix, rows, LANES), jnp.float32),
            pltpu.VMEM((radix * rows, 2 * LANES), jnp.float32),
            dma((halves,)), dma((halves,)),
            dma((chips,)), dma((chips,)), dma((chips,)), dma((chips,)), dma((chips,)), dma((chips,)),
            dma((halves,)), dma((halves,)), dma, dma, dma,
        ],
        compiler_params=pltpu.CompilerParams(collective_id=0, has_side_effects=True),
    )(
        voltages.reshape(2, tm, few, channels), beam_weights, station_map.reshape(1, stations),
        station_flags.reshape(1, stations), filter_taps, *tables(channels),
    )


def order_kernel(p_ref, o_ref, rows_ref):
    stn, beams, width = p_ref.shape
    radix = o_ref.shape[1]
    per_group = width // LANES
    cuts = LANES // radix
    for source in range(stn):
        for kk in range(per_group):
            rows_ref[pl.ds(source * per_group + kk, beams, stride=radix), :] = p_ref[
                source, :, kk * LANES : (kk + 1) * LANES
            ].astype(jnp.float32)
    row = lax.broadcasted_iota(jnp.int32, (LANES, LANES), 0)
    lane = lax.broadcasted_iota(jnp.int32, (LANES, LANES), 1)
    chosen = lax.rem(row, radix) * cuts + lax.div(row, radix)
    pick = jnp.where(lane == chosen, 1.0, 0.0).astype(jnp.bfloat16)
    turned = lax.dot_general(
        pick, rows_ref[...].astype(jnp.bfloat16), (((1,), (1,)), ((), ())), preferred_element_type=jnp.float32
    )
    place = lax.div(lax.broadcasted_iota(jnp.int32, (radix, LANES), 1), radix)
    for tile in range(beams * radix // LANES):
        parts = [turned[j * radix : (j + 1) * radix, tile * LANES : (tile + 1) * LANES] for j in range(cuts)]
        for bb in range(cuts):
            out = None
            for j in range(cuts):
                shift = (j - bb) % cuts * radix
                moved = pltpu.roll(parts[j], shift, 1) if shift else parts[j]
                out = moved if out is None else jnp.where(place == j, moved, out)
            o_ref[tile * cuts + bb] = out


def put_in_order(mine, radix):
    stn, beams, _ = mine.shape
    return pl.pallas_call(
        order_kernel,
        out_shape=jax.ShapeDtypeStruct((beams, radix, LANES), jnp.float32),
        in_specs=[pl.BlockSpec(memory_space=pltpu.VMEM)],
        out_specs=pl.BlockSpec(memory_space=pltpu.VMEM),
        scratch_shapes=[pltpu.VMEM((beams * radix, LANES), jnp.float32)],
    )(mine)


def on_device(tm_size, stn_size, voltages, filter_taps, beam_weights, station_map, station_flags):
    channels = filter_taps.shape[1]
    few = voltages.shape[1] // tm_size
    if few % 32 == 0 and stn_size % 2 == 0:
        mine = fused(tm_size, stn_size, voltages, filter_taps, beam_weights, station_map, station_flags)
        return put_in_order(mine, channels // LANES).reshape(mine.shape[1], 1, channels)
    else:
        weights = local_weights(beam_weights, station_map, station_flags, tm_size, stn_size)
        weight_all = lax.all_gather(weights, "stn", axis=1, tiled=True)
        frames = voltages.reshape(2, tm_size, few, channels)
        frames = lax.all_to_all(frames, "tm", split_axis=1, concat_axis=1, tiled=True)
        spectra = make_spectra(frames, filter_taps, stn_size)
        turned = lax.all_to_all(spectra, ("tm", "stn"), split_axis=0, concat_axis=0, tiled=True)
        power = make_power(turned, weight_all)
        beams = power.shape[0] // stn_size
        mine = lax.all_to_all(
            power.reshape(stn_size, beams, -1), "stn", split_axis=0, concat_axis=0, tiled=True
        )
    radix = channels // LANES
    mine = mine.reshape(stn_size, beams, radix // stn_size, LANES).astype(jnp.float32)
    return mine.transpose(1, 3, 0, 2).reshape(beams, 1, channels)


def solution(mesh):
    placed = (P(None, "stn", "tm"), P(), P(None, "stn", None), P(), P())
    body = functools.partial(on_device, mesh.shape["tm"], mesh.shape["stn"])
    return jax.shard_map(
        body, mesh=mesh, in_specs=placed, out_specs=P("stn", "tm", None), check_vma=False
    )
```
